256 devices in a mesh: train: 64 (over y, z, core), tile: 4 (over x).
Axes of the slice: x: 4, y: 4, z: 8, core: 2. Of those that a mesh axis runs over, the one named last changes fastest.
Arguments:
- test_grads: bfloat16 [8192, 4096], P('train', 'tile'), may hold values from -6 to 6
- fisher: bfloat16 [8, 512, 512], P('tile'), may hold values from -8 to 8
- train_grads: bfloat16 [262144, 4096], P(('train', 'tile')), may hold values from -0.09375 to 0.09375
- candidates: int32 [8192, 4], P('train'), may hold values from 0 to 63, all different within a row; in each aligned block of 128 rows (0 to 127, 128 to 255, ...) at most 12 rows name the same one
- shard_rows: int32 [64], P('train'), may hold values from 1024 to 4096
Outputs:
- top_scores: float32 [8192, 32], P('train')
The draws below stay inside these ranges and needn't reach their ends.
Inputs may be any that keep to these rules, and one draw needn't show every extreme that they name: `candidates`: each row names 4 different shards; among the rows of one index of train no shard is named by more than 12 rows.
All inputs are finite; a program needn't handle non-finite values.
Results may differ from the reference program's by a relative error of at most 0.0011.
Values may be sent and summed in bfloat16 or wider, within the bound.
No kernel may reach another device: no remote copies, remote signals or barrier semaphores. Data moves between devices by JAX's collectives and lax.ppermute only.
A program may use at most 128 MiB of HBM per device.

```python
import math
import jax
import jax.numpy as jnp
import numpy as np
from jax import lax

K = 4096
BLOCK = 512
NB = 8
Q_DEV = 128
CANDS = 4
TOPK = 32
CAP = 12
SLOTS = 768
SHARD = 4096
TESTS = 8192
TRAIN_ROWS = 262144
N_TRAIN = 64


def draw_fisher(key, part):
    first_key, second_key = jax.random.split(key, 2)
    offdiag = jnp.clip(jax.random.normal(first_key, (NB, BLOCK, BLOCK), jnp.float32), -4.0, 4.0) * (0.6 / math.sqrt(BLOCK))
    diagonal = jnp.exp(jax.random.uniform(second_key, (NB, BLOCK), jnp.float32, math.log(0.5), math.log(2.0)))
    identity = jnp.arange(BLOCK)[:, None] == jnp.arange(BLOCK)[None, :]
    blocks = jnp.where(identity[None, :, :], diagonal[:, :, None], offdiag)
    return blocks.astype(jnp.bfloat16)


def set_ends(drawn, rng, low, high):
    shape = drawn.shape
    spot = [jax.random.randint(jax.random.fold_in(rng, axis), (), 0, shape[axis]) for axis in range(len(shape))]
    drawn = drawn.at[tuple(spot)].set(low)
    longest = shape.index(max(shape))
    spot[longest] = (spot[longest] + 1) % shape[longest]
    return drawn.at[tuple(spot)].set(high)


def levels(stream_key, shape, cuts, least, high):
    gain, own = 1.0, jax.random.fold_in(stream_key, 6)
    for axis_at, shards_of in cuts:
        draws = jnp.exp(jax.random.uniform(jax.random.fold_in(own, axis_at), (shards_of,), jnp.float32, least / len(cuts), high / len(cuts)))
        gain = gain * jnp.repeat(draws, shape[axis_at] // shards_of).reshape([-1 if axis == axis_at else 1 for axis in range(len(shape))])
    return gain


def shared_out(stream_key, own, number, rows, count, top, bound, slope):
    order = jax.random.permutation(stream_key, count)
    crowded, ordinary = load_shares(count, rows * top, bound, slope, True), load_shares(count, rows * top, bound, slope, False)
    places = jnp.arange(count)

    def named(sizes, rotation):
        used = int((sizes > 0).sum())
        fixed = max(1, used // 4)
        passed = fixed + (places - fixed + rotation * (used - fixed)) % max(1, count - fixed)
        return jnp.zeros((count,), jnp.int32).at[order[jnp.where(places < fixed, places, passed)]].set(jnp.asarray(sizes, jnp.int32))

    sizes = jnp.where(number % 4 == 0, named(crowded, number // 4), named(ordinary, number - number // 4 - 1))
    mixed = jax.random.permutation(jax.random.fold_in(own, 3), count)
    donor, taker = mixed[0:count // 2 * 2:2], mixed[1:count // 2 * 2:2]
    slack = jnp.minimum(sizes[donor] - 1, bound - sizes[taker]) // 2
    slack = jnp.where((donor == order[0]) | (taker == order[0]) | (sizes[taker] == 0), 0, jnp.maximum(slack, 0))
    passed = jax.random.randint(jax.random.fold_in(own, 4), (count // 2,), 0, 1 << 20) % (slack + 1)
    sizes = sizes.at[donor].add(-passed).at[taker].add(passed)
    labels = jnp.searchsorted(jnp.cumsum(sizes), jnp.arange(rows * top), side="right").astype(jnp.int32)
    grid = labels.reshape(top, rows).T
    grid = grid[jax.random.permutation(jax.random.fold_in(own, 1), rows)]
    rotation = jax.random.randint(jax.random.fold_in(own, 2), (rows, 1), 0, top)
    return jnp.take_along_axis(grid, (jnp.arange(top)[None, :] + rotation) % top, axis=1)


def load_shares(amount, total, reach, skew, full):
    loads = [(1 << 20) // math.isqrt(grade ** skew) + 1 for grade in range(1, amount + 1)]
    largest = reach if full else min(reach, max(-(-total // amount), total * loads[0] // sum(loads)))
    least = 1 if total - largest >= amount - 1 else 0
    counts, surplus = [largest] + [least] * (amount - 1), total - largest - least * (amount - 1)
    while surplus > 0:
        free = [i for i in range(1, amount) if counts[i] < largest] or [i for i in range(1, amount) if counts[i] < reach]
        pool, remaining = sum([loads[i] for i in free]), surplus
        for i in free:
            more = min(reach - counts[i], max(1, remaining * loads[i] // pool), surplus)
            counts[i] = counts[i] + more
            surplus = surplus - more
    return np.array(counts)


def noise(own_key, dims, scale, limit, shards=(), held_as=jnp.bfloat16):
    result = scale * jax.random.normal(own_key, dims, jnp.float32)
    if shards:
        result = result * levels(own_key, dims, shards, -0.22, 0.18)
    return jnp.clip(result, -limit, limit).astype(held_as)


def setup_inputs(seed: int = 0) -> dict:
    key_list = jax.random.split(jax.random.key(seed), 6)
    test_grads = noise(key_list[0], (TESTS, K), 1.0, 6.0, ((0, 64), (1, 4)))
    fisher = draw_fisher(jax.random.fold_in(key_list[5], 71), 0)
    train_grads = noise(key_list[2], (TRAIN_ROWS, K), K ** -0.5, 0.09375, ((0, 256),))
    candidates_keys = jax.random.split(jax.random.fold_in(key_list[3], 1), TESTS // Q_DEV)
    candidates_turns = jax.random.permutation(jax.random.fold_in(key_list[3], 3), TESTS // Q_DEV)
    candidates = jax.vmap(lambda own, number: shared_out(jax.random.fold_in(key_list[3], 2), own, number, Q_DEV, N_TRAIN, CANDS, CAP, 2))(candidates_keys, candidates_turns).reshape((TESTS, CANDS))
    shard_rows = set_ends(jax.random.randint(key_list[4], (N_TRAIN,), SHARD // 4, SHARD + 1), jax.random.fold_in(key_list[4], 1), SHARD // 4, SHARD).astype(jnp.int32)
    return dict(test_grads=test_grads, fisher=fisher, train_grads=train_grads, candidates=candidates, shard_rows=shard_rows)


lowest_score = -1.0e30


def reference(test_grads, fisher, train_grads, candidates, shard_rows):
    test_count = test_grads.shape[0]
    blocks = fisher.shape[0]
    block_order = fisher.shape[1]
    precond = jnp.einsum("qbi,bij->qbj", test_grads.astype(jnp.float32).reshape(test_count, blocks, block_order), fisher.astype(jnp.float32))
    precond = precond.reshape(test_count, blocks * block_order).astype(jnp.bfloat16)
    padded = jnp.concatenate([precond.astype(jnp.float32), jnp.zeros((1, blocks * block_order), jnp.float32)], axis=0)
    shard_grads = train_grads.reshape(N_TRAIN, SHARD, K)

    def advance(leaders, inputs):
        shard_block, shard_id = inputs
        naming = jnp.any(candidates == shard_id, axis=1)
        picked = jnp.nonzero(naming, size=SLOTS, fill_value=test_count)[0].astype(jnp.int32)
        scores = jnp.dot(padded[picked], shard_block.astype(jnp.float32).T)
        alive_rows = jnp.arange(SHARD, dtype=jnp.int32) < shard_rows[shard_id]
        scores = jnp.where(alive_rows[None, :], scores, lowest_score)
        highest = lax.top_k(scores, TOPK)[0]
        merged = lax.top_k(jnp.concatenate([leaders[picked], highest], axis=1), TOPK)[0]
        return leaders.at[picked].set(merged), None

    initial = jnp.full((test_count + 1, TOPK), lowest_score, jnp.float32)
    leaders, _ = lax.scan(advance, initial, (shard_grads, jnp.arange(N_TRAIN, dtype=jnp.int32)))
    return leaders[:test_count]
```

```python
import functools

import jax
import jax.numpy as jnp
from jax import lax
from jax.experimental import pallas as pl
from jax.experimental.pallas import tpu as pltpu
from jax.sharding import PartitionSpec as P

TOPK = 32
LOWEST = -1.0e30
LANES = 128
SUBLANES = 8
ROW_BLOCK = TOPK * SUBLANES
WIDE, NARROW = 8, 4
VMEM_LIMIT = 56 * 1024 * 1024

f32, bf16, i32 = jnp.float32, jnp.bfloat16, jnp.int32


def iota(shape, dim):
    return lax.broadcasted_iota(i32, shape, dim)


def dot(a, b, dims=((1,), (0,))):
    return lax.dot_general(a, b, (dims, ((), ())), preferred_element_type=f32)


def sorting_pairs(n):
    pairs, p = [], 1
    while p < n:
        k = p
        while k >= 1:
            for j in range(k % p, n - k, 2 * k):
                for i in range(min(k, n - j - k)):
                    if (i + j) // (2 * p) == (i + j + k) // (2 * p):
                        pairs.append((i + j, i + j + k))
            k //= 2
        p *= 2
    return pairs


def exchange(v, i, j):
    v[i], v[j] = jnp.maximum(v[i], v[j]), jnp.minimum(v[i], v[j])


def sorted_down(v):
    v = list(v)
    for i, j in sorting_pairs(len(v)):
        exchange(v, i, j)
    return v


def bitonic_down(v):
    v, d = list(v), len(v) // 2
    while d:
        for i in range(len(v)):
            if not i & d:
                exchange(v, i, i + d)
        d //= 2
    return v


def best_of(a, b):
    return bitonic_down([jnp.maximum(x, y) for x, y in zip(a, reversed(b))])


def bitonic_rows(x, down):
    v = [x[i : i + SUBLANES] for i in range(0, TOPK, SUBLANES)]
    row = iota((SUBLANES, LANES), 0)
    for d in (2, 1):
        for i in range(len(v)):
            if not i & d:
                high, low = jnp.maximum(v[i], v[i + d]), jnp.minimum(v[i], v[i + d])
                v[i], v[i + d] = (high, low) if down else (low, high)
    for d in (4, 2, 1):
        first = (row & d) == 0
        for i, y in enumerate(v):
            after, before = pltpu.roll(y, SUBLANES - d, 0), pltpu.roll(y, d, 0)
            if down:
                v[i] = jnp.where(first, jnp.maximum(y, after), jnp.minimum(y, before))
            else:
                v[i] = jnp.where(first, jnp.minimum(y, after), jnp.maximum(y, before))
    return jnp.concatenate(v, axis=0)


def dispatch_kernel(grads_ref, fisher_ref, cand_ref, first_ref, second_ref, rank_ref):
    q_rows = grads_ref.shape[0]
    blocks, order, _ = fisher_ref.shape
    shards_n = first_ref.shape[0] // WIDE
    precond = jnp.concatenate(
        [
            dot(grads_ref[:, b * order : (b + 1) * order], fisher_ref[b]).astype(bf16)
            for b in range(blocks)
        ],
        axis=1,
    )
    half = blocks * order // 2
    cand = cand_ref[...]
    shard = iota((shards_n, q_rows), 0)
    naming = [cand[c : c + 1, :] == shard for c in range(cand.shape[0])]
    named = functools.reduce(jnp.logical_or, naming)
    before = (iota((q_rows, q_rows), 0) < iota((q_rows, q_rows), 1)).astype(f32).astype(bf16)
    rank = dot(named.astype(f32).astype(bf16), before)
    for c, here in enumerate(naming):
        at = jnp.sum(jnp.where(here, rank, 0.0), axis=0, keepdims=True)
        rank_ref[c : c + 1, :] = at.astype(i32)
    table = jnp.where(named, rank, 255.0).astype(bf16)
    rows = shards_n * WIDE
    spread = (iota((rows, shards_n), 0) // WIDE == iota((rows, shards_n), 1)).astype(f32)
    place = dot(spread.astype(bf16), table)
    row = iota((rows, q_rows), 0)
    pick = (place == (row % WIDE).astype(f32)).astype(f32).astype(bf16)
    first_ref[...] = dot(pick, precond).astype(bf16)
    pick = (place == (row % NARROW + WIDE).astype(f32)).astype(f32).astype(bf16)
    both = dot(pick, precond)
    upper = iota((rows, half), 0) // NARROW % 2 == 0
    second_ref[...] = jnp.where(upper, both[:, :half], both[:, half:]).astype(bf16)


def unfold_kernel(folded_ref, rows_ref):
    half = folded_ref.shape[1]
    upper = iota((SUBLANES, half), 0) < NARROW
    for i in range(0, rows_ref.shape[0], 2 * SUBLANES):
        x = folded_ref[2 * i : 2 * i + 4 * SUBLANES, :].astype(f32)
        built = []
        for k in (0, 2):
            a = x[k * SUBLANES : (k + 1) * SUBLANES]
            b = x[(k + 1) * SUBLANES : (k + 2) * SUBLANES]
            left = jnp.where(upper, a, pltpu.roll(b, NARROW, 0))
            right = jnp.where(upper, pltpu.roll(a, NARROW, 0), b)
            built.append(jnp.concatenate([left, right], axis=1))
        rows_ref[i : i + 2 * SUBLANES, :] = jnp.concatenate(built, axis=0).astype(bf16)


def score_kernel(slots, meta_ref, train_ref, *refs):
    q_refs, (out_ref, sum_ref, top_ref, turned_ref) = refs[:-4], refs[-4:]
    step = pl.program_id(0)
    me, live = meta_ref[0], meta_ref[1]
    width = train_ref.shape[1] // 4
    groups = sum_ref.shape[1] // LANES
    sources = out_ref.shape[0]

    @pl.when(step == 0)
    def _():
        top_ref[...] = jnp.full(top_ref.shape, LOWEST, f32)

    for j, pair in enumerate(q_refs[i : i + 2] for i in range(0, 8, 2)):
        away = (0, 3, 1, 2)[j]
        column = pl.multiple_of(((me + away) & 3) * width, width)
        q = jnp.concatenate([ref[...] for ref in pair], axis=0)
        part = dot(train_ref[:, pl.ds(column, width)], q, ((1,), (1,)))
        sum_ref[...] = part if j == 0 else sum_ref[...] + part

    row = iota((SUBLANES, LANES), 0) + step * ROW_BLOCK

    def group(g, carry):
        lanes = pl.ds(pl.multiple_of(g * LANES, LANES), LANES)
        v = []
        for k in range(TOPK):
            x = sum_ref[k * SUBLANES : (k + 1) * SUBLANES, lanes]
            v.append(jnp.where(row + k * SUBLANES < live, x, LOWEST))
        v = sorted_down(v)
        v = best_of(v, [top_ref[g, k] for k in range(TOPK)])
        for k in range(TOPK):
            top_ref[g, k] = v[k]
        return carry

    lax.fori_loop(0, groups, group, 0)

    @pl.when(step == pl.num_programs(0) - 1)
    def _():
        sub = iota((SUBLANES, LANES), 0)

        def finish(g, carry):
            v = [top_ref[g, k] for k in range(TOPK)]
            for d in (4, 2, 1):
                v = best_of(v, [pltpu.roll(x, d, 0) for x in v])
            tiles = []
            for i in range(0, TOPK, SUBLANES):
                x = v[i]
                for k in range(1, SUBLANES):
                    x = jnp.where(sub == k, v[i + k], x)
                tiles.append(x)
            tiles = jnp.concatenate(tiles * (LANES // TOPK), axis=0)
            turned_ref[pl.ds(pl.multiple_of(g * LANES, LANES), LANES), :] = tiles.T
            return carry

        lax.fori_loop(0, groups, finish, 0)
        lane = iota((sources, LANES), 1) // TOPK
        per = LANES // TOPK
        for i in range(0, slots, per):
            built = turned_ref[pl.ds(i, sources, stride=slots), :]
            for k in range(1, per):
                x = turned_ref[pl.ds(i + k, sources, stride=slots), :]
                built = jnp.where(lane == k, x, built)
            out_ref[:, i * TOPK : (i + per) * TOPK] = built


def home_kernel(wide_ref, narrow_ref, cand_ref, rank_ref, down_ref, up_ref):
    sources = wide_ref.shape[0]
    returned = jnp.concatenate([wide_ref[...], narrow_ref[...]], axis=1)
    parts, rest = [], returned
    for _ in range(3):
        parts.append(rest.astype(bf16))
        rest = rest - parts[-1].astype(f32)
    cand, rank = cand_ref[...], rank_ref[...]
    shard = iota((sources, LANES), 0)
    flip = (iota((TOPK, TOPK), 0) + iota((TOPK, TOPK), 1) == TOPK - 1).astype(f32).astype(bf16)

    def chosen(c, backwards):
        mine = (cand[c : c + 1, :] == shard).astype(f32).astype(bf16)
        split = []
        for part in parts:
            all_ranks = dot(part, mine, ((0,), (0,)))
            best = all_ranks[:TOPK]
            for r in range(1, WIDE + NARROW):
                best = jnp.where(rank[c : c + 1, :] == r, all_ranks[r * TOPK : (r + 1) * TOPK], best)
            split.append(dot(flip, best.astype(bf16)) if backwards else best)
        return split[0] + split[1] + split[2]

    one = bitonic_rows(jnp.maximum(chosen(0, False), chosen(1, True)), True)
    two = bitonic_rows(jnp.maximum(chosen(2, False), chosen(3, True)), False)
    joined = jnp.maximum(one, two)
    down_ref[...] = bitonic_rows(joined, True)
    up_ref[...] = bitonic_rows(joined, False)


def final_kernel(a_ref, b_ref, c_ref, d_ref, out_ref):
    one = bitonic_rows(jnp.maximum(a_ref[...], b_ref[...]), True)
    two = bitonic_rows(jnp.maximum(c_ref[...], d_ref[...]), False)
    best = bitonic_rows(jnp.maximum(one, two), True)
    turned = jnp.concatenate([best] * (LANES // TOPK), axis=0).T
    out_ref[...] = turned[:, :TOPK]


def shift(x, axis, by):
    n = lax.axis_size(axis)
    return lax.ppermute(x, axis, [(i, (i + by) % n) for i in range(n)])


def exchange_train(x):
    return lax.all_to_all(x, "train", split_axis=0, concat_axis=0, tiled=True)


def over_tiles(x):
    n = x.shape[0] // 2
    a, b = x[:n], x[n:]
    left_a, right_b = shift(a, "tile", 1), shift(b, "tile", -1)
    left_b, right_a = shift(b, "tile", 1), shift(a, "tile", -1)
    far_a, far_b = shift(left_a, "tile", 1), shift(right_b, "tile", -1)
    return a, b, left_a, left_b, right_a, right_b, far_a, far_b


def call(kernel, shapes, **kwargs):
    return pl.pallas_call(
        kernel,
        out_shape=shapes,
        compiler_params=pltpu.CompilerParams(vmem_limit_bytes=VMEM_LIMIT),
        **kwargs,
    )


def scores(meta, train_grads, q, slots, sources):
    rows, features = train_grads.shape
    columns = slots * sources
    whole = [pl.BlockSpec(x.shape, lambda i: (0, 0)) for x in q]
    return pl.pallas_call(
        functools.partial(score_kernel, slots),
        out_shape=jax.ShapeDtypeStruct((sources, slots * TOPK), f32),
        grid=(rows // ROW_BLOCK,),
        in_specs=[
            pl.BlockSpec(memory_space=pltpu.SMEM),
            pl.BlockSpec((ROW_BLOCK, features), lambda i: (i, 0)),
            *whole,
        ],
        out_specs=pl.BlockSpec((sources, slots * TOPK), lambda i: (0, 0)),
        scratch_shapes=[
            pltpu.VMEM((ROW_BLOCK, columns), f32),
            pltpu.VMEM((columns // LANES, TOPK, SUBLANES, LANES), f32),
            pltpu.VMEM((columns, LANES), f32),
        ],
        compiler_params=pltpu.CompilerParams(vmem_limit_bytes=VMEM_LIMIT),
    )(meta, train_grads, *q)


def shards(test_grads, fisher, train_grads, candidates, shard_rows):
    sources = lax.axis_size("train")
    q_rows, features = test_grads.shape
    cand = candidates.T
    cand_count = cand.shape[0]
    me = lax.axis_index("tile")
    meta = jnp.stack([me.astype(i32), shard_rows[0] - me * train_grads.shape[0]])
    first, second, rank = call(
        dispatch_kernel,
        (
            jax.ShapeDtypeStruct((sources * WIDE, features), bf16),
            jax.ShapeDtypeStruct((sources * WIDE, features // 2), bf16),
            jax.ShapeDtypeStruct((cand_count, q_rows), i32),
        ),
    )(test_grads, fisher, cand)
    first = exchange_train(first.reshape(sources, WIDE, features))
    second = exchange_train(second.reshape(sources, WIDE, features // 2))
    wide = over_tiles(first.reshape(sources * WIDE, features))
    second = call(unfold_kernel, jax.ShapeDtypeStruct((sources * NARROW, features), bf16))(
        second.reshape(sources * WIDE, features // 2)
    )
    narrow = over_tiles(second)
    wide = scores(meta, train_grads, wide, WIDE, sources)
    narrow = scores(meta, train_grads, narrow, NARROW, sources)
    wide = exchange_train(wide)
    narrow = exchange_train(narrow)
    best = jax.ShapeDtypeStruct((TOPK, q_rows), f32)
    down, up = call(home_kernel, (best, best))(wide, narrow, cand, rank)
    return call(final_kernel, jax.ShapeDtypeStruct((q_rows, TOPK), f32))(
        down, shift(up, "tile", 1), shift(down, "tile", 2), shift(up, "tile", 3)
    )


def solution(mesh):
    placed = (
        P("train", "tile"),
        P("tile", None, None),
        P(("train", "tile"), None),
        P("train", None),
        P("train"),
    )
    return jax.shard_map(
        shards, mesh=mesh, in_specs=placed, out_specs=P("train", None), check_vma=False
    )
```

```python
import functools

import jax
import jax.numpy as jnp
from jax import lax
from jax.experimental import pallas as pl
from jax.experimental.pallas import tpu as pltpu
from jax.sharding import PartitionSpec as P

TOPK = 32
LOWEST = -1.0e30
LANES = 128
SUBLANES = 8
ROW_BLOCK = TOPK * SUBLANES
WIDE, NARROW = 8, 4
VMEM_LIMIT = 12 * 1024 * 1024

f32, bf16, i32 = jnp.float32, jnp.bfloat16, jnp.int32


def iota(shape, dim):
    return lax.broadcasted_iota(i32, shape, dim)


def dot(a, b, dims=((1,), (0,))):
    return lax.dot_general(a, b, (dims, ((), ())), preferred_element_type=f32)


def sorting_pairs(n):
    pairs, p = [], 1
    while p < n:
        k = p
        while k >= 1:
            for j in range(k % p, n - k, 2 * k):
                for i in range(min(k, n - j - k)):
                    if (i + j) // (2 * p) == (i + j + k) // (2 * p):
                        pairs.append((i + j, i + j + k))
            k //= 2
        p *= 2
    return pairs


def exchange(v, i, j):
    v[i], v[j] = jnp.maximum(v[i], v[j]), jnp.minimum(v[i], v[j])


def sorted_down(v):
    v = list(v)
    for i, j in sorting_pairs(len(v)):
        exchange(v, i, j)
    return v


def bitonic_down(v):
    v, d = list(v), len(v) // 2
    while d:
        for i in range(len(v)):
            if not i & d:
                exchange(v, i, i + d)
        d //= 2
    return v


def best_of(a, b):
    return bitonic_down([jnp.maximum(x, y) for x, y in zip(a, reversed(b))])


def bitonic_rows(x, down):
    v = [x[i : i + SUBLANES] for i in range(0, TOPK, SUBLANES)]
    row = iota((SUBLANES, LANES), 0)
    for d in (2, 1):
        for i in range(len(v)):
            if not i & d:
                high, low = jnp.maximum(v[i], v[i + d]), jnp.minimum(v[i], v[i + d])
                v[i], v[i + d] = (high, low) if down else (low, high)
    for d in (4, 2, 1):
        first = (row & d) == 0
        for i, y in enumerate(v):
            after, before = pltpu.roll(y, SUBLANES - d, 0), pltpu.roll(y, d, 0)
            if down:
                v[i] = jnp.where(first, jnp.maximum(y, after), jnp.minimum(y, before))
            else:
                v[i] = jnp.where(first, jnp.minimum(y, after), jnp.maximum(y, before))
    return jnp.concatenate(v, axis=0)


def dispatch_kernel(
    grads_hbm, fisher_hbm, cand_hbm, first_ref, second_ref, rank_ref, grads_ref, fisher_ref, cand_ref, arrived
):
    copies = [
        pltpu.make_async_copy(source, target, arrived.at[k])
        for k, (source, target) in enumerate(
            ((fisher_hbm, fisher_ref), (grads_hbm, grads_ref), (cand_hbm, cand_ref))
        )
    ]
    for copy in copies:
        copy.start()
    for copy in copies:
        copy.wait()
    q_rows = grads_ref.shape[0]
    blocks, order, _ = fisher_ref.shape
    shards_n = first_ref.shape[0] // WIDE
    precond = jnp.concatenate(
        [
            dot(grads_ref[:, b * order : (b + 1) * order], fisher_ref[b]).astype(bf16)
            for b in range(blocks)
        ],
        axis=1,
    )
    half = blocks * order // 2
    cand = cand_ref[...]
    shard = iota((shards_n, q_rows), 0)
    naming = [cand[c : c + 1, :] == shard for c in range(cand.shape[0])]
    named = functools.reduce(jnp.logical_or, naming)
    before = (iota((q_rows, q_rows), 0) < iota((q_rows, q_rows), 1)).astype(f32).astype(bf16)
    rank = dot(named.astype(f32).astype(bf16), before)
    for c, here in enumerate(naming):
        at = jnp.sum(jnp.where(here, rank, 0.0), axis=0, keepdims=True)
        rank_ref[c : c + 1, :] = at.astype(i32)
    table = jnp.where(named, rank, 255.0).astype(bf16)
    rows = shards_n * WIDE
    spread = (iota((rows, shards_n), 0) // WIDE == iota((rows, shards_n), 1)).astype(f32)
    place = dot(spread.astype(bf16), table)
    row = iota((rows, q_rows), 0)
    pick = (place == (row % WIDE).astype(f32)).astype(f32).astype(bf16)
    first_ref[...] = dot(pick, precond).astype(bf16)
    pick = (place == (row % NARROW + WIDE).astype(f32)).astype(f32).astype(bf16)
    both = dot(pick, precond)
    upper = iota((rows, half), 0) // NARROW % 2 == 0
    second_ref[...] = jnp.where(upper, both[:, :half], both[:, half:]).astype(bf16)


def unfold_kernel(folded_ref, left_ref, right_ref, rows_ref, up_ref, down_ref):
    half = folded_ref.shape[1]
    ahead = left_ref.shape[0] // 2
    upper = iota((SUBLANES, half), 0) < NARROW
    for i in range(0, rows_ref.shape[0], 2 * SUBLANES):
        x = folded_ref[2 * i : 2 * i + 4 * SUBLANES, :].astype(f32)
        built = []
        for k in (0, 2):
            a = x[k * SUBLANES : (k + 1) * SUBLANES]
            b = x[(k + 1) * SUBLANES : (k + 2) * SUBLANES]
            left = jnp.where(upper, a, pltpu.roll(b, NARROW, 0))
            right = jnp.where(upper, pltpu.roll(a, NARROW, 0), b)
            built.append(jnp.concatenate([left, right], axis=1))
        built = jnp.concatenate(built, axis=0).astype(bf16)
        rows_ref[i : i + 2 * SUBLANES, :] = built
        up_ref[ahead + i : ahead + i + 2 * SUBLANES, :] = built
        down_ref[ahead + i : ahead + i + 2 * SUBLANES, :] = built
    up_ref[:ahead, :] = left_ref[:ahead, :]
    down_ref[:ahead, :] = right_ref[ahead:, :]


AWAY = (0, 3, 1, 2)


def partial_kernel(meta_ref, rows_ref, own_ref, left_ref, right_ref, train_ref, sum_ref, arrived):
    me = meta_ref[0]
    width = train_ref.shape[2]
    copies = []
    for j, away in enumerate(AWAY):
        columns = pl.ds(pl.multiple_of(((me + away) & 3) * width, width), width)
        copies.append(
            pltpu.make_async_copy(rows_ref.at[:, columns], train_ref.at[j], arrived.at[j])
        )
        copies[-1].start()
    total = None
    for j, ref in enumerate((own_ref, left_ref, right_ref)):
        copies[j].wait()
        part = dot(train_ref[j], ref[...], ((1,), (1,)))
        total = part if total is None else total + part
    sum_ref[...] = total
    copies[3].wait()


def select(slots, live, sum_ref, turned_ref, write):
    rows, columns = sum_ref.shape
    sources = columns // slots
    sub = iota((SUBLANES, LANES), 0)

    def group(g, carry):
        lanes = pl.ds(pl.multiple_of(g * LANES, LANES), LANES)
        best = None
        for i in range(0, rows, ROW_BLOCK):
            v = []
            for k in range(i, i + ROW_BLOCK, SUBLANES):
                v.append(jnp.where(sub < live - k, sum_ref[k : k + SUBLANES, lanes], LOWEST))
            v = sorted_down(v)
            best = v if best is None else best_of(best, v)
        for d in (4, 2, 1):
            best = best_of(best, [pltpu.roll(x, d, 0) for x in best])
        tiles = []
        for i in range(0, TOPK, SUBLANES):
            x = best[i]
            for k in range(1, SUBLANES):
                x = jnp.where(sub == k, best[i + k], x)
            tiles.append(x)
        tiles = jnp.concatenate(tiles * (LANES // TOPK), axis=0)
        turned_ref[pl.ds(pl.multiple_of(g * LANES, LANES), LANES), :] = tiles.T
        return carry

    lax.fori_loop(0, columns // LANES, group, 0)
    lane = iota((sources, LANES), 1) // TOPK
    per = LANES // TOPK
    for i in range(0, slots, per):
        built = turned_ref[pl.ds(i, sources, stride=slots), :]
        for k in range(1, per):
            x = turned_ref[pl.ds(i + k, sources, stride=slots), :]
            built = jnp.where(lane == k, x, built)
        write(i * TOPK, built)


def wide_kernel(meta_ref, train_ref, part_ref, up_ref, down_ref, out_ref, sum_ref, turned_ref):
    half = sum_ref.shape[1] // 2
    for k, ref in enumerate((up_ref, down_ref)):
        at = slice(k * half, (k + 1) * half)
        sum_ref[:, at] = part_ref[:, at] + dot(train_ref[3], ref[:half, :], ((1,), (1,)))

    def write(at, built):
        out_ref[:, at : at + LANES] = built

    select(WIDE, meta_ref[1], sum_ref, turned_ref, write)


def narrow_kernel(
    meta_ref, train_ref, own_ref, up_ref, down_ref, far_a_ref, far_b_ref, wide_ref, out_ref, sum_ref, turned_ref
):
    skip = up_ref.shape[0] - sum_ref.shape[1]
    far = jnp.concatenate([far_a_ref[...], far_b_ref[...]], axis=0)
    blocks = (own_ref[...], up_ref[skip:, :], down_ref[skip:, :], far)
    sum_ref[...] = functools.reduce(
        jnp.add, [dot(train_ref[j], q, ((1,), (1,))) for j, q in enumerate(blocks)]
    )
    done = wide_ref.shape[1]
    out_ref[:, 0, :done] = wide_ref[...]

    def write(at, built):
        out_ref[:, 0, done + at : done + at + LANES] = built

    select(NARROW, meta_ref[1], sum_ref, turned_ref, write)


def turned_over(x):
    v = [x[i : i + SUBLANES] for i in range(TOPK - SUBLANES, -1, -SUBLANES)]
    row = iota((SUBLANES, LANES), 0)
    for d in (4, 2, 1):
        first = (row & d) == 0
        v = [jnp.where(first, pltpu.roll(y, SUBLANES - d, 0), pltpu.roll(y, d, 0)) for y in v]
    return jnp.concatenate(v, axis=0)


def home_kernel(returned_ref, cand_ref, rank_ref, down_ref, up_ref):
    sources = returned_ref.shape[0]
    rest = returned_ref[:, 0, :]
    cand, rank = cand_ref[...], rank_ref[...]
    shard = iota((sources, LANES), 0)
    mine = jnp.concatenate(
        [(cand[c : c + 1, :] == shard).astype(f32).astype(bf16) for c in range(cand.shape[0])], axis=1
    )
    found = None
    for _ in range(3):
        part = rest.astype(bf16)
        rest = rest - part.astype(f32)
        x = dot(part, mine, ((0,), (0,)))
        found = x if found is None else found + x

    def chosen(c):
        at = slice(c * LANES, (c + 1) * LANES)
        best = found[:TOPK, at]
        for r in range(1, WIDE + NARROW):
            best = jnp.where(rank[c : c + 1, :] == r, found[r * TOPK : (r + 1) * TOPK, at], best)
        return best

    one = bitonic_rows(jnp.maximum(chosen(0), turned_over(chosen(1))), True)
    two = bitonic_rows(jnp.maximum(chosen(2), turned_over(chosen(3))), False)
    joined = jnp.maximum(one, two)
    down_ref[...] = bitonic_rows(joined, True)
    up_ref[...] = bitonic_rows(joined, False)


def final_kernel(a_ref, b_ref, c_ref, d_ref, out_ref):
    one = bitonic_rows(jnp.maximum(a_ref[...], b_ref[...]), True)
    two = bitonic_rows(jnp.maximum(c_ref[...], d_ref[...]), False)
    out_ref[...] = bitonic_rows(jnp.maximum(one, two), True)


def shift(x, axis, by):
    n = lax.axis_size(axis)
    return lax.ppermute(x, axis, [(i, (i + by) % n) for i in range(n)])


def exchange_train(x):
    return lax.all_to_all(x, "train", split_axis=0, concat_axis=0, tiled=True)


def near(x):
    return shift(x, "tile", 1), shift(x, "tile", -1)


SMEM, HBM, VMEM = (pl.BlockSpec(memory_space=x) for x in (pltpu.SMEM, pltpu.HBM, pltpu.VMEM))


def call(kernel, shapes, *operands, spaces=None, scratch=(), limit=VMEM_LIMIT):
    spaces = [VMEM] * len(operands) if spaces is None else spaces
    return pl.pallas_call(
        kernel,
        out_shape=shapes,
        in_specs=spaces,
        out_specs=jax.tree.map(lambda _: VMEM, shapes),
        scratch_shapes=scratch,
        compiler_params=pltpu.CompilerParams(vmem_limit_bytes=limit),
    )(*operands)


def in_hbm(x):
    return pltpu.with_memory_space_constraint(x, pltpu.HBM)


def shards(test_grads, fisher, train_grads, candidates, shard_rows):
    sources = lax.axis_size("train")
    q_rows, features = test_grads.shape
    rows = train_grads.shape[0]
    cand = candidates.T
    me = lax.axis_index("tile")
    meta = jnp.stack([me.astype(i32), shard_rows[0] - me * rows])
    array = jax.ShapeDtypeStruct
    first, second, rank = call(
        dispatch_kernel,
        (
            array((sources * WIDE, features), bf16),
            array((sources * WIDE, features // 2), bf16),
            array(cand.shape, i32),
        ),
        in_hbm(test_grads),
        in_hbm(fisher),
        in_hbm(cand),
        spaces=[HBM] * 3,
        scratch=[
            pltpu.VMEM(test_grads.shape, bf16),
            pltpu.VMEM(fisher.shape, bf16),
            pltpu.VMEM(cand.shape, i32),
            pltpu.SemaphoreType.DMA((3,)),
        ],
    )
    first = exchange_train(first.reshape(sources, WIDE, features))
    second, first = lax.optimization_barrier((second, first))
    second = exchange_train(second.reshape(sources, WIDE, features // 2))
    first = first.reshape(sources * WIDE, features)
    left, right = near(first)
    second, left, right = lax.optimization_barrier((second, left, right))
    doubled = array((2 * sources * NARROW, features), bf16)
    second, up, down = call(
        unfold_kernel,
        (array((sources * NARROW, features), bf16), doubled, doubled),
        second.reshape(sources * WIDE, features // 2),
        left,
        right,
    )
    after, _ = lax.optimization_barrier((meta, second))
    up, down = shift(up, "tile", 1), shift(down, "tile", -1)
    train, part = call(
        partial_kernel,
        (array((4, rows, features), bf16), array((rows, sources * WIDE), f32)),
        after,
        in_hbm(train_grads),
        first,
        left,
        right,
        spaces=[SMEM, HBM, VMEM, VMEM, VMEM],
        scratch=[pltpu.SemaphoreType.DMA((4,))],
    )
    up, down, part = lax.optimization_barrier((up, down, part))
    start, middle = sources * NARROW, sources * (NARROW + NARROW // 2)
    ends = shift(up[start:middle], "tile", 1), shift(down[middle:], "tile", -1)

    def room(slots):
        columns = slots * sources
        return [pltpu.VMEM((rows, columns), f32), pltpu.VMEM((columns, LANES), f32)]

    wide = call(
        wide_kernel,
        array((sources, WIDE * TOPK), f32),
        meta,
        train,
        part,
        up,
        down,
        spaces=[SMEM] + [VMEM] * 4,
        scratch=room(WIDE),
    )
    both = call(
        narrow_kernel,
        array((sources, 1, (WIDE + NARROW) * TOPK), f32),
        meta,
        train,
        second,
        up,
        down,
        *ends,
        wide,
        spaces=[SMEM] + [VMEM] * 7,
        scratch=room(NARROW),
    )
    both = exchange_train(both)
    best = array((TOPK, q_rows), f32)
    down, up = call(home_kernel, (best, best), both, cand, rank)
    return call(
        final_kernel, best, down, shift(up, "tile", 1), shift(down, "tile", 2), shift(up, "tile", 3)
    ).T


def solution(mesh):
    placed = (
        P("train", "tile"),
        P("tile", None, None),
        P(("train", "tile"), None),
        P("train", None),
        P("train"),
    )
    return jax.shard_map(
        shards, mesh=mesh, in_specs=placed, out_specs=P("train", None), check_vma=False
    )
```

```python
import functools

import jax
import jax.numpy as jnp
from jax import lax
from jax.experimental import pallas as pl
from jax.experimental.pallas import tpu as pltpu
from jax.sharding import PartitionSpec as P

TOPK = 32
LOWEST = -1.0e30
LANES = 128
SUBLANES = 8
ROW_BLOCK = TOPK * SUBLANES
WIDE, NARROW = 8, 4
VMEM_LIMIT = 12 * 1024 * 1024

f32, bf16, i32 = jnp.float32, jnp.bfloat16, jnp.int32


def iota(shape, dim):
    return lax.broadcasted_iota(i32, shape, dim)


def dot(a, b, dims=((1,), (0,))):
    return lax.dot_general(a, b, (dims, ((), ())), preferred_element_type=f32)


def sorting_pairs(n):
    pairs, p = [], 1
    while p < n:
        k = p
        while k >= 1:
            for j in range(k % p, n - k, 2 * k):
                for i in range(min(k, n - j - k)):
                    if (i + j) // (2 * p) == (i + j + k) // (2 * p):
                        pairs.append((i + j, i + j + k))
            k //= 2
        p *= 2
    return pairs


def exchange(v, i, j):
    v[i], v[j] = jnp.maximum(v[i], v[j]), jnp.minimum(v[i], v[j])


def sorted_down(v):
    v = list(v)
    for i, j in sorting_pairs(len(v)):
        exchange(v, i, j)
    return v


def bitonic_down(v):
    v, d = list(v), len(v) // 2
    while d:
        for i in range(len(v)):
            if not i & d:
                exchange(v, i, i + d)
        d //= 2
    return v


def best_of(a, b):
    return bitonic_down([jnp.maximum(x, y) for x, y in zip(a, reversed(b))])


def bitonic_rows(x, down):
    v = [x[i : i + SUBLANES] for i in range(0, TOPK, SUBLANES)]
    row = iota((SUBLANES, LANES), 0)
    for d in (2, 1):
        for i in range(len(v)):
            if not i & d:
                high, low = jnp.maximum(v[i], v[i + d]), jnp.minimum(v[i], v[i + d])
                v[i], v[i + d] = (high, low) if down else (low, high)
    for d in (4, 2, 1):
        first = (row & d) == 0
        for i, y in enumerate(v):
            after, before = pltpu.roll(y, SUBLANES - d, 0), pltpu.roll(y, d, 0)
            if down:
                v[i] = jnp.where(first, jnp.maximum(y, after), jnp.minimum(y, before))
            else:
                v[i] = jnp.where(first, jnp.minimum(y, after), jnp.maximum(y, before))
    return jnp.concatenate(v, axis=0)


def dispatch_kernel(
    grads_hbm, fisher_hbm, cand_hbm, first_ref, second_ref, rank_ref, grads_ref, fisher_ref, cand_ref, arrived
):
    copies = [
        pltpu.make_async_copy(source, target, arrived.at[k])
        for k, (source, target) in enumerate(
            ((fisher_hbm, fisher_ref), (grads_hbm, grads_ref), (cand_hbm, cand_ref))
        )
    ]
    for copy in copies:
        copy.start()
    for copy in copies:
        copy.wait()
    q_rows = grads_ref.shape[0]
    blocks, order, _ = fisher_ref.shape
    shards_n = first_ref.shape[0] // WIDE
    precond = jnp.concatenate(
        [
            dot(grads_ref[:, b * order : (b + 1) * order], fisher_ref[b]).astype(bf16)
            for b in range(blocks)
        ],
        axis=1,
    )
    half = blocks * order // 2
    cand = cand_ref[...]
    shard = iota((shards_n, q_rows), 0)
    naming = [cand[c : c + 1, :] == shard for c in range(cand.shape[0])]
    named = functools.reduce(jnp.logical_or, naming)
    before = (iota((q_rows, q_rows), 0) < iota((q_rows, q_rows), 1)).astype(f32).astype(bf16)
    rank = dot(named.astype(f32).astype(bf16), before)
    for c, here in enumerate(naming):
        at = jnp.sum(jnp.where(here, rank, 0.0), axis=0, keepdims=True)
        rank_ref[c : c + 1, :] = at.astype(i32)
    table = jnp.where(named, rank, 255.0).astype(bf16)
    rows = shards_n * WIDE
    spread = (iota((rows, shards_n), 0) // WIDE == iota((rows, shards_n), 1)).astype(f32)
    place = dot(spread.astype(bf16), table)
    row = iota((rows, q_rows), 0)
    pick = (place == (row % WIDE).astype(f32)).astype(f32).astype(bf16)
    first_ref[...] = dot(pick, precond).astype(bf16)
    pick = (place == (row % NARROW + WIDE).astype(f32)).astype(f32).astype(bf16)
    both = dot(pick, precond)
    upper = iota((rows, half), 0) // NARROW % 2 == 0
    second_ref[...] = jnp.where(upper, both[:, :half], both[:, half:]).astype(bf16)


def unfold_kernel(folded_ref, rows_ref):
    half = folded_ref.shape[1]
    upper = iota((SUBLANES, half), 0) < NARROW
    for i in range(0, rows_ref.shape[0], 2 * SUBLANES):
        x = folded_ref[2 * i : 2 * i + 4 * SUBLANES, :].astype(f32)
        built = []
        for k in (0, 2):
            a = x[k * SUBLANES : (k + 1) * SUBLANES]
            b = x[(k + 1) * SUBLANES : (k + 2) * SUBLANES]
            left = jnp.where(upper, a, pltpu.roll(b, NARROW, 0))
            right = jnp.where(upper, pltpu.roll(a, NARROW, 0), b)
            built.append(jnp.concatenate([left, right], axis=1))
        rows_ref[i : i + 2 * SUBLANES, :] = jnp.concatenate(built, axis=0).astype(bf16)


AWAY = (0, 3, 1, 2)


def partial_kernel(meta_ref, rows_ref, *refs):
    q_refs, (train_ref, sum_ref, arrived) = refs[:-3], refs[-3:]
    me = meta_ref[0]
    width = train_ref.shape[2]
    half = sum_ref.shape[1] // 2
    copies = []
    for j, away in enumerate(AWAY):
        columns = pl.ds(pl.multiple_of(((me + away) & 3) * width, width), width)
        copies.append(
            pltpu.make_async_copy(rows_ref.at[:, columns], train_ref.at[j], arrived.at[j])
        )
        copies[-1].start()
    for j, copy in enumerate(copies[:3]):
        copy.wait()
        for k in range(2):
            at = slice(k * half, (k + 1) * half)
            part = dot(train_ref[j], q_refs[2 * j + k][...], ((1,), (1,)))
            sum_ref[:, at] = part if j == 0 else sum_ref[:, at] + part
    copies[3].wait()


def select(slots, live, sum_ref, turned_ref, write):
    rows, columns = sum_ref.shape
    sources = columns // slots
    sub = iota((SUBLANES, LANES), 0)

    def group(g, carry):
        lanes = pl.ds(pl.multiple_of(g * LANES, LANES), LANES)
        best = None
        for i in range(0, rows, ROW_BLOCK):
            v = []
            for k in range(i, i + ROW_BLOCK, SUBLANES):
                v.append(jnp.where(sub < live - k, sum_ref[k : k + SUBLANES, lanes], LOWEST))
            v = sorted_down(v)
            best = v if best is None else best_of(best, v)
        for d in (4, 2, 1):
            best = best_of(best, [pltpu.roll(x, d, 0) for x in best])
        tiles = []
        for i in range(0, TOPK, SUBLANES):
            x = best[i]
            for k in range(1, SUBLANES):
                x = jnp.where(sub == k, best[i + k], x)
            tiles.append(x)
        tiles = jnp.concatenate(tiles * (LANES // TOPK), axis=0)
        turned_ref[pl.ds(pl.multiple_of(g * LANES, LANES), LANES), :] = tiles.T
        return carry

    lax.fori_loop(0, columns // LANES, group, 0)
    lane = iota((sources, LANES), 1) // TOPK
    per = LANES // TOPK
    for i in range(0, slots, per):
        built = turned_ref[pl.ds(i, sources, stride=slots), :]
        for k in range(1, per):
            x = turned_ref[pl.ds(i + k, sources, stride=slots), :]
            built = jnp.where(lane == k, x, built)
        write(i * TOPK, built)


def wide_kernel(meta_ref, train_ref, part_ref, far_a_ref, far_b_ref, out_ref, sum_ref, turned_ref):
    half = sum_ref.shape[1] // 2
    for k, ref in enumerate((far_a_ref, far_b_ref)):
        at = slice(k * half, (k + 1) * half)
        sum_ref[:, at] = part_ref[:, at] + dot(train_ref[3], ref[...], ((1,), (1,)))

    def write(at, built):
        out_ref[:, at : at + LANES] = built

    select(WIDE, meta_ref[1], sum_ref, turned_ref, write)


def narrow_partial_kernel(train_ref, own_ref, left_ref, right_ref, sum_ref):
    total = None
    for j, ref in enumerate((own_ref, left_ref, right_ref)):
        part = dot(train_ref[j], ref[...], ((1,), (1,)))
        total = part if total is None else total + part
    sum_ref[...] = total


def narrow_kernel(
    meta_ref, train_ref, part_ref, far_a_ref, far_b_ref, wide_ref, out_ref, sum_ref, turned_ref
):
    far = jnp.concatenate([far_a_ref[...], far_b_ref[...]], axis=0)
    sum_ref[...] = part_ref[...] + dot(train_ref[3], far, ((1,), (1,)))
    done = wide_ref.shape[1]
    out_ref[:, 0, :done] = wide_ref[...]

    def write(at, built):
        out_ref[:, 0, done + at : done + at + LANES] = built

    select(NARROW, meta_ref[1], sum_ref, turned_ref, write)


def turned_over(x):
    v = [x[i : i + SUBLANES] for i in range(TOPK - SUBLANES, -1, -SUBLANES)]
    row = iota((SUBLANES, LANES), 0)
    for d in (4, 2, 1):
        first = (row & d) == 0
        v = [jnp.where(first, pltpu.roll(y, SUBLANES - d, 0), pltpu.roll(y, d, 0)) for y in v]
    return jnp.concatenate(v, axis=0)


def home_kernel(returned_ref, cand_ref, rank_ref, down_ref, up_ref):
    sources = returned_ref.shape[0]
    rest = returned_ref[:, 0, :]
    cand, rank = cand_ref[...], rank_ref[...]
    shard = iota((sources, LANES), 0)
    mine = jnp.concatenate(
        [(cand[c : c + 1, :] == shard).astype(f32).astype(bf16) for c in range(cand.shape[0])], axis=1
    )
    found = None
    for _ in range(3):
        part = rest.astype(bf16)
        rest = rest - part.astype(f32)
        x = dot(part, mine, ((0,), (0,)))
        found = x if found is None else found + x

    def chosen(c):
        at = slice(c * LANES, (c + 1) * LANES)
        best = found[:TOPK, at]
        for r in range(1, WIDE + NARROW):
            best = jnp.where(rank[c : c + 1, :] == r, found[r * TOPK : (r + 1) * TOPK, at], best)
        return best

    one = bitonic_rows(jnp.maximum(chosen(0), turned_over(chosen(1))), True)
    two = bitonic_rows(jnp.maximum(chosen(2), turned_over(chosen(3))), False)
    joined = jnp.maximum(one, two)
    down_ref[...] = bitonic_rows(joined, True)
    up_ref[...] = bitonic_rows(joined, False)


def final_kernel(a_ref, b_ref, c_ref, d_ref, out_ref):
    one = bitonic_rows(jnp.maximum(a_ref[...], b_ref[...]), True)
    two = bitonic_rows(jnp.maximum(c_ref[...], d_ref[...]), False)
    out_ref[...] = bitonic_rows(jnp.maximum(one, two), True)


def shift(x, axis, by):
    n = lax.axis_size(axis)
    return lax.ppermute(x, axis, [(i, (i + by) % n) for i in range(n)])


def exchange_train(x):
    return lax.all_to_all(x, "train", split_axis=0, concat_axis=0, tiled=True)


def near(x):
    return shift(x, "tile", 1), shift(x, "tile", -1)


SMEM, HBM, VMEM = (pl.BlockSpec(memory_space=x) for x in (pltpu.SMEM, pltpu.HBM, pltpu.VMEM))


def call(kernel, shapes, *operands, spaces=None, scratch=(), limit=VMEM_LIMIT):
    spaces = [VMEM] * len(operands) if spaces is None else spaces
    return pl.pallas_call(
        kernel,
        out_shape=shapes,
        in_specs=spaces,
        out_specs=jax.tree.map(lambda _: VMEM, shapes),
        scratch_shapes=scratch,
        compiler_params=pltpu.CompilerParams(vmem_limit_bytes=limit),
    )(*operands)


def halves(left, right):
    n = left.shape[0] // 2
    return left[:n], right[n:]


def far(left, right):
    return shift(left, "tile", 1), shift(right, "tile", -1)


def in_hbm(x):
    return pltpu.with_memory_space_constraint(x, pltpu.HBM)


def shards(test_grads, fisher, train_grads, candidates, shard_rows):
    sources = lax.axis_size("train")
    q_rows, features = test_grads.shape
    rows = train_grads.shape[0]
    cand = candidates.T
    me = lax.axis_index("tile")
    meta = jnp.stack([me.astype(i32), shard_rows[0] - me * rows])
    array = jax.ShapeDtypeStruct
    first, second, rank = call(
        dispatch_kernel,
        (
            array((sources * WIDE, features), bf16),
            array((sources * WIDE, features // 2), bf16),
            array(cand.shape, i32),
        ),
        in_hbm(test_grads),
        in_hbm(fisher),
        in_hbm(cand),
        spaces=[HBM] * 3,
        scratch=[
            pltpu.VMEM(test_grads.shape, bf16),
            pltpu.VMEM(fisher.shape, bf16),
            pltpu.VMEM(cand.shape, i32),
            pltpu.SemaphoreType.DMA((3,)),
        ],
    )
    first = exchange_train(first.reshape(sources, WIDE, features))
    first = first.reshape(sources * WIDE, features)
    n = first.shape[0] // 2
    own_a, own_b = first[:n], first[n:]
    second, own_a, own_b = lax.optimization_barrier((second, own_a, own_b))
    second = exchange_train(second.reshape(sources, WIDE, features // 2))
    left_a, right_b = shift(own_a, "tile", 1), shift(own_b, "tile", -1)
    left_a, right_b, own_a, own_b = lax.optimization_barrier((left_a, right_b, own_a, own_b))
    left_b, right_a = shift(own_b, "tile", 1), shift(own_a, "tile", -1)
    wide_far = far(left_a, right_b)
    second, own_a, own_b = lax.optimization_barrier((second, own_a, own_b))
    second = call(
        unfold_kernel,
        array((sources * NARROW, features), bf16),
        second.reshape(sources * WIDE, features // 2),
    )
    second_left, second_right = near(second)
    train, part = call(
        partial_kernel,
        (array((4, rows, features), bf16), array((rows, sources * WIDE), f32)),
        meta,
        in_hbm(train_grads),
        own_a,
        own_b,
        left_a,
        left_b,
        right_a,
        right_b,
        spaces=[SMEM, HBM] + [VMEM] * 6,
        scratch=[pltpu.SemaphoreType.DMA((4,))],
    )
    def room(slots):
        columns = slots * sources
        return [pltpu.VMEM((rows, columns), f32), pltpu.VMEM((columns, LANES), f32)]

    wide = call(
        wide_kernel,
        array((sources, WIDE * TOPK), f32),
        meta,
        train,
        part,
        *wide_far,
        spaces=[SMEM] + [VMEM] * 4,
        scratch=room(WIDE),
    )
    left, right, wide = lax.optimization_barrier((second_left, second_right, wide))
    narrow_far = far(*halves(left, right))
    narrow_part = call(
        narrow_partial_kernel,
        array((rows, sources * NARROW), f32),
        train,
        second,
        left,
        right,
    )

    wide, narrow_part, *narrow_far = lax.optimization_barrier((wide, narrow_part, *narrow_far))
    both = call(
        narrow_kernel,
        array((sources, 1, (WIDE + NARROW) * TOPK), f32),
        meta,
        train,
        narrow_part,
        *narrow_far,
        wide,
        spaces=[SMEM] + [VMEM] * 5,
        scratch=room(NARROW),
    )
    both = exchange_train(both)
    best = array((TOPK, q_rows), f32)
    down, up = call(home_kernel, (best, best), both, cand, rank)
    return call(
        final_kernel, best, down, shift(up, "tile", 1), shift(down, "tile", 2), shift(up, "tile", 3)
    ).T


def solution(mesh):
    placed = (
        P("train", "tile"),
        P("tile", None, None),
        P(("train", "tile"), None),
        P("train", None),
        P("train"),
    )
    return jax.shard_map(
        shards, mesh=mesh, in_specs=placed, out_specs=P("train", None), check_vma=False
    )
```

```python
import functools

import jax
import jax.numpy as jnp
from jax import lax
from jax.experimental import pallas as pl
from jax.experimental.pallas import tpu as pltpu
from jax.sharding import PartitionSpec as P

TOPK = 32
LOWEST = -1.0e30
LANES = 128
SUBLANES = 8
ROW_BLOCK = TOPK * SUBLANES
WIDE, NARROW = 8, 4
VMEM_LIMIT = 12 * 1024 * 1024

f32, bf16, i32 = jnp.float32, jnp.bfloat16, jnp.int32


def iota(shape, dim):
    return lax.broadcasted_iota(i32, shape, dim)


def dot(a, b, dims=((1,), (0,))):
    return lax.dot_general(a, b, (dims, ((), ())), preferred_element_type=f32)


def sorting_pairs(n):
    pairs, p = [], 1
    while p < n:
        k = p
        while k >= 1:
            for j in range(k % p, n - k, 2 * k):
                for i in range(min(k, n - j - k)):
                    if (i + j) // (2 * p) == (i + j + k) // (2 * p):
                        pairs.append((i + j, i + j + k))
            k //= 2
        p *= 2
    return pairs


def exchange(v, i, j):
    v[i], v[j] = jnp.maximum(v[i], v[j]), jnp.minimum(v[i], v[j])


def sorted_down(v):
    v = list(v)
    for i, j in sorting_pairs(len(v)):
        exchange(v, i, j)
    return v


def bitonic_down(v):
    v, d = list(v), len(v) // 2
    while d:
        for i in range(len(v)):
            if not i & d:
                exchange(v, i, i + d)
        d //= 2
    return v


def best_of(a, b):
    return bitonic_down([jnp.maximum(x, y) for x, y in zip(a, reversed(b))])


def bitonic_rows(x, down):
    v = [x[i : i + SUBLANES] for i in range(0, TOPK, SUBLANES)]
    row = iota((SUBLANES, LANES), 0)
    for d in (2, 1):
        for i in range(len(v)):
            if not i & d:
                high, low = jnp.maximum(v[i], v[i + d]), jnp.minimum(v[i], v[i + d])
                v[i], v[i + d] = (high, low) if down else (low, high)
    for d in (4, 2, 1):
        first = (row & d) == 0
        for i, y in enumerate(v):
            after, before = pltpu.roll(y, SUBLANES - d, 0), pltpu.roll(y, d, 0)
            if down:
                v[i] = jnp.where(first, jnp.maximum(y, after), jnp.minimum(y, before))
            else:
                v[i] = jnp.where(first, jnp.minimum(y, after), jnp.maximum(y, before))
    return jnp.concatenate(v, axis=0)


def dispatch_kernel(
    grads_hbm, fisher_hbm, cand_hbm, first_ref, second_ref, rank_ref, grads_ref, fisher_ref, cand_ref, arrived
):
    copies = [
        pltpu.make_async_copy(source, target, arrived.at[k])
        for k, (source, target) in enumerate(
            ((fisher_hbm, fisher_ref), (grads_hbm, grads_ref), (cand_hbm, cand_ref))
        )
    ]
    for copy in copies:
        copy.start()
    for copy in copies:
        copy.wait()
    q_rows = grads_ref.shape[0]
    blocks, order, _ = fisher_ref.shape
    shards_n = first_ref.shape[0] // WIDE
    precond = jnp.concatenate(
        [
            dot(grads_ref[:, b * order : (b + 1) * order], fisher_ref[b]).astype(bf16)
            for b in range(blocks)
        ],
        axis=1,
    )
    half = blocks * order // 2
    cand = cand_ref[...]
    shard = iota((shards_n, q_rows), 0)
    naming = [cand[c : c + 1, :] == shard for c in range(cand.shape[0])]
    named = functools.reduce(jnp.logical_or, naming)
    before = (iota((q_rows, q_rows), 0) < iota((q_rows, q_rows), 1)).astype(f32).astype(bf16)
    rank = dot(named.astype(f32).astype(bf16), before)
    for c, here in enumerate(naming):
        at = jnp.sum(jnp.where(here, rank, 0.0), axis=0, keepdims=True)
        rank_ref[c : c + 1, :] = at.astype(i32)
    table = jnp.where(named, rank, 255.0).astype(bf16)
    rows = shards_n * WIDE
    spread = (iota((rows, shards_n), 0) // WIDE == iota((rows, shards_n), 1)).astype(f32)
    place = dot(spread.astype(bf16), table)
    row = iota((rows, q_rows), 0)
    pick = (place == (row % WIDE).astype(f32)).astype(f32).astype(bf16)
    first_ref[...] = dot(pick, precond).astype(bf16)
    pick = (place == (row % NARROW + WIDE).astype(f32)).astype(f32).astype(bf16)
    both = dot(pick, precond)
    upper = iota((rows, half), 0) // NARROW % 2 == 0
    second_ref[...] = jnp.where(upper, both[:, :half], both[:, half:]).astype(bf16)


def unfold_kernel(folded_ref, rows_ref):
    half = folded_ref.shape[1]
    upper = iota((SUBLANES, half), 0) < NARROW
    for i in range(0, rows_ref.shape[0], 2 * SUBLANES):
        x = folded_ref[2 * i : 2 * i + 4 * SUBLANES, :].astype(f32)
        built = []
        for k in (0, 2):
            a = x[k * SUBLANES : (k + 1) * SUBLANES]
            b = x[(k + 1) * SUBLANES : (k + 2) * SUBLANES]
            left = jnp.where(upper, a, pltpu.roll(b, NARROW, 0))
            right = jnp.where(upper, pltpu.roll(a, NARROW, 0), b)
            built.append(jnp.concatenate([left, right], axis=1))
        rows_ref[i : i + 2 * SUBLANES, :] = jnp.concatenate(built, axis=0).astype(bf16)


AWAY = (0, 3, 1, 2)


def partial_kernel(meta_ref, rows_ref, *refs):
    q_refs, (train_ref, sum_ref, arrived) = refs[:-3], refs[-3:]
    me = meta_ref[0]
    width = train_ref.shape[2]
    half = sum_ref.shape[1] // 2
    copies = []
    for j, away in enumerate(AWAY):
        columns = pl.ds(pl.multiple_of(((me + away) & 3) * width, width), width)
        copies.append(
            pltpu.make_async_copy(rows_ref.at[:, columns], train_ref.at[j], arrived.at[j])
        )
        copies[-1].start()
    for j, copy in enumerate(copies[:3]):
        copy.wait()
        for k in range(2):
            at = slice(k * half, (k + 1) * half)
            part = dot(train_ref[j], q_refs[2 * j + k][...], ((1,), (1,)))
            sum_ref[:, at] = part if j == 0 else sum_ref[:, at] + part
    copies[3].wait()


def select(slots, live, sum_ref, turned_ref, write):
    rows, columns = sum_ref.shape
    sources = columns // slots
    sub = iota((SUBLANES, LANES), 0)

    def group(g, carry):
        lanes = pl.ds(pl.multiple_of(g * LANES, LANES), LANES)
        best = None
        for i in range(0, rows, ROW_BLOCK):
            v = []
            for k in range(i, i + ROW_BLOCK, SUBLANES):
                v.append(jnp.where(sub < live - k, sum_ref[k : k + SUBLANES, lanes], LOWEST))
            v = sorted_down(v)
            best = v if best is None else best_of(best, v)
        for d in (4, 2, 1):
            best = best_of(best, [pltpu.roll(x, d, 0) for x in best])
        tiles = []
        for i in range(0, TOPK, SUBLANES):
            x = best[i]
            for k in range(1, SUBLANES):
                x = jnp.where(sub == k, best[i + k], x)
            tiles.append(x)
        tiles = jnp.concatenate(tiles * (LANES // TOPK), axis=0)
        turned_ref[pl.ds(pl.multiple_of(g * LANES, LANES), LANES), :] = tiles.T
        return carry

    lax.fori_loop(0, columns // LANES, group, 0)
    lane = iota((sources, LANES), 1) // TOPK
    per = LANES // TOPK
    for i in range(0, slots, per):
        built = turned_ref[pl.ds(i, sources, stride=slots), :]
        for k in range(1, per):
            x = turned_ref[pl.ds(i + k, sources, stride=slots), :]
            built = jnp.where(lane == k, x, built)
        write(i * TOPK, built)


def wide_kernel(meta_ref, train_ref, part_ref, far_a_ref, far_b_ref, out_ref, sum_ref, turned_ref):
    half = sum_ref.shape[1] // 2
    for k, ref in enumerate((far_a_ref, far_b_ref)):
        at = slice(k * half, (k + 1) * half)
        sum_ref[:, at] = part_ref[:, at] + dot(train_ref[3], ref[...], ((1,), (1,)))

    def write(at, built):
        out_ref[:, at : at + LANES] = built

    select(WIDE, meta_ref[1], sum_ref, turned_ref, write)


def narrow_partial_kernel(train_ref, own_ref, left_ref, right_ref, sum_ref):
    total = None
    for j, ref in enumerate((own_ref, left_ref, right_ref)):
        part = dot(train_ref[j], ref[...], ((1,), (1,)))
        total = part if total is None else total + part
    sum_ref[...] = total


def narrow_kernel(
    meta_ref, train_ref, part_ref, far_a_ref, far_b_ref, wide_ref, out_ref, sum_ref, turned_ref
):
    far = jnp.concatenate([far_a_ref[...], far_b_ref[...]], axis=0)
    sum_ref[...] = part_ref[...] + dot(train_ref[3], far, ((1,), (1,)))
    done = wide_ref.shape[1]
    out_ref[:, 0, :done] = wide_ref[...]

    def write(at, built):
        out_ref[:, 0, done + at : done + at + LANES] = built

    select(NARROW, meta_ref[1], sum_ref, turned_ref, write)


def turned_over(x):
    v = [x[i : i + SUBLANES] for i in range(TOPK - SUBLANES, -1, -SUBLANES)]
    row = iota((SUBLANES, LANES), 0)
    for d in (4, 2, 1):
        first = (row & d) == 0
        v = [jnp.where(first, pltpu.roll(y, SUBLANES - d, 0), pltpu.roll(y, d, 0)) for y in v]
    return jnp.concatenate(v, axis=0)


def home_kernel(returned_ref, cand_ref, rank_ref, down_ref, up_ref):
    sources = returned_ref.shape[0]
    rest = returned_ref[:, 0, :]
    cand, rank = cand_ref[...], rank_ref[...]
    shard = iota((sources, LANES), 0)
    mine = jnp.concatenate(
        [(cand[c : c + 1, :] == shard).astype(f32).astype(bf16) for c in range(cand.shape[0])], axis=1
    )
    found = None
    for _ in range(3):
        part = rest.astype(bf16)
        rest = rest - part.astype(f32)
        x = dot(part, mine, ((0,), (0,)))
        found = x if found is None else found + x

    def chosen(c):
        at = slice(c * LANES, (c + 1) * LANES)
        best = found[:TOPK, at]
        for r in range(1, WIDE + NARROW):
            best = jnp.where(rank[c : c + 1, :] == r, found[r * TOPK : (r + 1) * TOPK, at], best)
        return best

    one = bitonic_rows(jnp.maximum(chosen(0), turned_over(chosen(1))), True)
    two = bitonic_rows(jnp.maximum(chosen(2), turned_over(chosen(3))), False)
    joined = jnp.maximum(one, two)
    down_ref[...] = bitonic_rows(joined, True)
    up_ref[...] = bitonic_rows(joined, False)


def final_kernel(a_ref, b_ref, c_ref, d_ref, out_ref):
    one = bitonic_rows(jnp.maximum(a_ref[...], b_ref[...]), True)
    two = bitonic_rows(jnp.maximum(c_ref[...], d_ref[...]), False)
    out_ref[...] = bitonic_rows(jnp.maximum(one, two), True)


def shift(x, axis, by):
    n = lax.axis_size(axis)
    return lax.ppermute(x, axis, [(i, (i + by) % n) for i in range(n)])


def exchange_train(x):
    return lax.all_to_all(x, "train", split_axis=0, concat_axis=0, tiled=True)


def near(x):
    return shift(x, "tile", 1), shift(x, "tile", -1)


SMEM, HBM, VMEM = (pl.BlockSpec(memory_space=x) for x in (pltpu.SMEM, pltpu.HBM, pltpu.VMEM))


def call(kernel, shapes, *operands, spaces=None, scratch=(), limit=VMEM_LIMIT):
    spaces = [VMEM] * len(operands) if spaces is None else spaces
    return pl.pallas_call(
        kernel,
        out_shape=shapes,
        in_specs=spaces,
        out_specs=jax.tree.map(lambda _: VMEM, shapes),
        scratch_shapes=scratch,
        compiler_params=pltpu.CompilerParams(vmem_limit_bytes=limit),
    )(*operands)


def halves(left, right):
    n = left.shape[0] // 2
    return left[:n], right[n:]


def far(left, right):
    return shift(left, "tile", 1), shift(right, "tile", -1)


def in_hbm(x):
    return pltpu.with_memory_space_constraint(x, pltpu.HBM)


def shards(test_grads, fisher, train_grads, candidates, shard_rows):
    sources = lax.axis_size("train")
    q_rows, features = test_grads.shape
    rows = train_grads.shape[0]
    cand = candidates.T
    me = lax.axis_index("tile")
    meta = jnp.stack([me.astype(i32), shard_rows[0] - me * rows])
    array = jax.ShapeDtypeStruct
    first, second, rank = call(
        dispatch_kernel,
        (
            array((sources * WIDE, features), bf16),
            array((sources * WIDE, features // 2), bf16),
            array(cand.shape, i32),
        ),
        in_hbm(test_grads),
        in_hbm(fisher),
        in_hbm(cand),
        spaces=[HBM] * 3,
        scratch=[
            pltpu.VMEM(test_grads.shape, bf16),
            pltpu.VMEM(fisher.shape, bf16),
            pltpu.VMEM(cand.shape, i32),
            pltpu.SemaphoreType.DMA((3,)),
        ],
    )
    first = exchange_train(first.reshape(sources, WIDE, features))
    first = first.reshape(sources * WIDE, features)
    n = first.shape[0] // 2
    own_a, own_b = first[:n], first[n:]
    second, own_a, own_b = lax.optimization_barrier((second, own_a, own_b))
    second = exchange_train(second.reshape(sources, WIDE, features // 2))
    left_a, right_b = shift(own_a, "tile", 1), shift(own_b, "tile", -1)
    left_a, right_b, own_a, own_b = lax.optimization_barrier((left_a, right_b, own_a, own_b))
    left_b, right_a = shift(own_b, "tile", 1), shift(own_a, "tile", -1)
    wide_far = far(left_a, right_b)
    second, own_a, own_b = lax.optimization_barrier((second, own_a, own_b))
    second = call(
        unfold_kernel,
        array((sources * NARROW, features), bf16),
        second.reshape(sources * WIDE, features // 2),
    )
    second_left, second_right = near(second)
    train, part = call(
        partial_kernel,
        (array((4, rows, features), bf16), array((rows, sources * WIDE), f32)),
        meta,
        in_hbm(train_grads),
        own_a,
        own_b,
        left_a,
        left_b,
        right_a,
        right_b,
        spaces=[SMEM, HBM] + [VMEM] * 6,
        scratch=[pltpu.SemaphoreType.DMA((4,))],
    )
    def room(slots):
        columns = slots * sources
        turned = pltpu.VMEM((columns + SUBLANES, LANES), f32)
        return [pltpu.VMEM((rows, columns), f32), turned]

    wide = call(
        wide_kernel,
        array((sources, WIDE * TOPK), f32),
        meta,
        train,
        part,
        *wide_far,
        spaces=[SMEM] + [VMEM] * 4,
        scratch=room(WIDE),
    )
    left, right, wide = lax.optimization_barrier((second_left, second_right, wide))
    narrow_far = far(*halves(left, right))
    narrow_part = call(
        narrow_partial_kernel,
        array((rows, sources * NARROW), f32),
        train,
        second,
        left,
        right,
    )

    wide, narrow_part, *narrow_far = lax.optimization_barrier((wide, narrow_part, *narrow_far))
    both = call(
        narrow_kernel,
        array((sources, 1, (WIDE + NARROW) * TOPK), f32),
        meta,
        train,
        narrow_part,
        *narrow_far,
        wide,
        spaces=[SMEM] + [VMEM] * 5,
        scratch=room(NARROW),
    )
    both = exchange_train(both)
    best = array((TOPK, q_rows), f32)
    down, up = call(home_kernel, (best, best), both, cand, rank)
    return call(
        final_kernel, best, down, shift(up, "tile", 1), shift(down, "tile", 2), shift(up, "tile", 3)
    ).T


def solution(mesh):
    placed = (
        P("train", "tile"),
        P("tile", None, None),
        P(("train", "tile"), None),
        P("train", None),
        P("train"),
    )
    return jax.shard_map(
        shards, mesh=mesh, in_specs=placed, out_specs=P("train", None), check_vma=False
    )
```
